512 devices in a mesh: box: 32 (over z, x_hi, core), dir: 16 (over x_lo, y).
Axes of the slice: x: 4 (x_hi: 2, x_lo: 2; x = x_hi * 2 + x_lo), y: 8, z: 8, core: 2. Of those that a mesh axis runs over, the one named last changes fastest.
Arguments:
- patterns: float32 [2048, 2, 1, 8192], P('box', None, None, 'dir'), may hold values from -6 to 6
- translators: float32 [316, 2, 8192], P(None, None, 'dir'), may hold values from -1.25 to 1.25
- send_rows: int32 [32, 32, 6], P('box'), may hold values from 0 to 63, as said below
- far_slot: int32 [2048, 24], P('box'), may hold values from 0 to 191
- far_offset: int32 [2048, 24], P('box'), may hold values from 0 to 315
- far_count: int32 [2048], P('box'), may hold values from 1 to 24, as said below
- children: int32 [512, 4], P('box'), may hold values from 0 to 2047, as said below
- octant: int32 [2048], P('box'), may hold values from 0 to 7
Outputs:
- received: float32 [2048, 2, 1, 8192], P('box', None, None, 'dir')
- upward: float32 [512, 2, 1, 32768], P('box', None, None, 'dir')
The draws below stay inside these ranges and needn't reach their ends.
Inputs may be any that keep to these rules, and one draw needn't show every extreme that they name: `send_rows`: within each sender and receiver pair the 6 rows are distinct local rows of the sender. `far_count`: every device's boxes have between 1 and 24 live entries; some box has exactly 24. The children of a coarser box owned by box device d are rows of that same device; every finer box is the child of exactly one coarser box.
All inputs are finite; a program needn't handle non-finite values.
Results may differ from the reference program's by a relative error of at most 0.0003.
Values sent between devices are 32-bit elements; how exact they have to be, the bound alone decides.
A program may use at most 128 MiB of HBM per device.

```python
import jax
import jax.numpy as jnp
from jax import lax

THETA0 = 64
PHI0 = 128
THETA1 = 128
PHI1 = 256
FIELDS = 1
CH = 4
NOFF = 316
FAR = 24
SLOT = 6
BOX_DEV0 = 64
NB0 = 2048
K0 = 8192
N_BOX = 32


def draw_send_rows(key, part):
    rand_keys = jax.random.split(jax.random.fold_in(key, 11), N_BOX * N_BOX)
    perm_rows = jax.vmap(lambda sub_key: jax.random.permutation(sub_key, BOX_DEV0)[:SLOT])(rand_keys)
    return perm_rows.reshape(N_BOX, N_BOX, SLOT).astype(jnp.int32)


def draw_far_count(key, part):
    first_key, second_key, third_key = jax.random.split(jax.random.fold_in(key, 23), 3)
    upper_bound = jax.random.randint(first_key, (N_BOX, 1), FAR // 4, FAR + 1)
    raw_ints = jax.random.randint(second_key, (N_BOX, BOX_DEV0), 0, 1 << 20)
    counts = (1 + raw_ints % upper_bound).reshape(-1)
    peak_spot = jax.random.randint(third_key, (), 0, N_BOX * BOX_DEV0)
    return counts.at[peak_spot].set(FAR).astype(jnp.int32)


def draw_children(key, part):
    rand_keys = jax.random.split(jax.random.fold_in(key, 37), N_BOX)
    perm_rows = jax.vmap(lambda sub_key: jax.random.permutation(sub_key, BOX_DEV0))(rand_keys)
    row_base = (jnp.arange(N_BOX, dtype=jnp.int32) * BOX_DEV0)[:, None]
    return (perm_rows + row_base).reshape(N_BOX * BOX_DEV0 // CH, CH).astype(jnp.int32)


def place_ends(entries, own_key, smallest, largest):
    index_at = [jax.random.randint(jax.random.fold_in(own_key, axis), (), 0, length) for axis, length in enumerate(entries.shape)]
    widest = entries.shape.index(max(entries.shape))
    neighbour = index_at[:widest] + [(index_at[widest] + 1) % entries.shape[widest]] + index_at[widest + 1:]
    return entries.at[tuple(index_at)].set(smallest).at[tuple(neighbour)].set(largest)


def shard_levels(stream_key, extent, shards, least, largest):
    gain, own = 1.0, jax.random.fold_in(stream_key, 6)
    for axis_at, shards_of in shards:
        draws = jnp.exp(jax.random.uniform(jax.random.fold_in(own, axis_at), (shards_of,), jnp.float32, least / len(shards), largest / len(shards)))
        gain = gain * jnp.repeat(draws, extent[axis_at] // shards_of).reshape([-1 if axis == axis_at else 1 for axis in range(len(extent))])
    return gain


def gaussian(stream_key, extent, scale, most, cuts=(), held_as=jnp.bfloat16):
    result = scale * jax.random.normal(stream_key, extent, jnp.float32)
    if cuts:
        result = result * shard_levels(stream_key, extent, cuts, -0.22, 0.18)
    return jnp.clip(result, -most, most).astype(held_as)


def setup_inputs(seed: int = 0) -> dict:
    arg_keys = jax.random.split(jax.random.key(seed), 9)
    return {
        "patterns": gaussian(arg_keys[0], (NB0, 2, FIELDS, K0), 1.0, 6.0, ((0, 32), (3, 16)), jnp.float32),
        "translators": gaussian(arg_keys[1], (NOFF, 2, K0), FAR ** -0.5, 1.25, ((2, 16),), jnp.float32),
        "send_rows": draw_send_rows(jax.random.fold_in(arg_keys[8], 71), 0),
        "far_slot": place_ends(jax.random.randint(arg_keys[3], (NB0, FAR), 0, N_BOX * SLOT), jax.random.fold_in(arg_keys[3], 1), 0, (N_BOX * SLOT) - 1).astype(jnp.int32),
        "far_offset": place_ends(jax.random.randint(arg_keys[4], (NB0, FAR), 0, NOFF), jax.random.fold_in(arg_keys[4], 1), 0, NOFF - 1).astype(jnp.int32),
        "far_count": draw_far_count(jax.random.fold_in(arg_keys[8], 71), 0),
        "children": draw_children(jax.random.fold_in(arg_keys[8], 71), 0),
        "octant": place_ends(jax.random.randint(arg_keys[7], (NB0,), 0, 8), jax.random.fold_in(arg_keys[7], 1), 0, 7).astype(jnp.int32),
    }


HALF_PHASE = 8.0


def theta_matrix(fine_count, coarse_count):
    fine_angle = jnp.pi * (jnp.arange(fine_count, dtype=jnp.float32) + 0.5) / fine_count
    coarse_angle = jnp.pi * (jnp.arange(coarse_count, dtype=jnp.float32) + 0.5) / coarse_count
    orders = jnp.arange(coarse_count, dtype=jnp.float32)
    weights = jnp.where(orders > 0.5, 2.0, 1.0).astype(jnp.float32)
    fine_cos = jnp.cos(fine_angle[:, None] * orders[None, :]) * weights[None, :]
    coarse_cos = jnp.cos(coarse_angle[:, None] * orders[None, :])
    return jnp.dot(fine_cos, coarse_cos.T, precision=lax.Precision.HIGHEST) / coarse_count


def phi_matrix(fine_count, coarse_count):
    fine_angle = 2.0 * jnp.pi * jnp.arange(fine_count, dtype=jnp.float32) / fine_count
    coarse_angle = 2.0 * jnp.pi * jnp.arange(coarse_count, dtype=jnp.float32) / coarse_count
    half_count = coarse_count // 2
    orders = jnp.arange(half_count + 1, dtype=jnp.float32)
    weights = jnp.where(orders < 0.5, 1.0, jnp.where(orders > half_count - 0.5, 1.0, 2.0)).astype(jnp.float32)
    fine_cos = jnp.cos(fine_angle[:, None] * orders[None, :]) * weights[None, :]
    fine_sin = jnp.sin(fine_angle[:, None] * orders[None, :]) * weights[None, :]
    coarse_cos = jnp.cos(coarse_angle[:, None] * orders[None, :])
    coarse_sin = jnp.sin(coarse_angle[:, None] * orders[None, :])
    total = jnp.dot(fine_cos, coarse_cos.T, precision=lax.Precision.HIGHEST)
    total = total + jnp.dot(fine_sin, coarse_sin.T, precision=lax.Precision.HIGHEST)
    return total / coarse_count


def phase_tables(octants):
    theta_fine = jnp.pi * (jnp.arange(THETA1, dtype=jnp.float32) + 0.5) / THETA1
    phi_fine = 2.0 * jnp.pi * jnp.arange(PHI1, dtype=jnp.float32) / PHI1
    unit_x = (jnp.sin(theta_fine)[:, None] * jnp.cos(phi_fine)[None, :]).reshape(-1)
    unit_y = (jnp.sin(theta_fine)[:, None] * jnp.sin(phi_fine)[None, :]).reshape(-1)
    unit_z = (jnp.cos(theta_fine)[:, None] * jnp.ones((PHI1,), jnp.float32)[None, :]).reshape(-1)
    sign_x = 1.0 - 2.0 * (octants % 2).astype(jnp.float32)
    sign_y = 1.0 - 2.0 * ((octants // 2) % 2).astype(jnp.float32)
    sign_z = 1.0 - 2.0 * ((octants // 4) % 2).astype(jnp.float32)
    angle = HALF_PHASE * (sign_x[:, None] * unit_x[None, :] + sign_y[:, None] * unit_y[None, :] + sign_z[:, None] * unit_z[None, :])
    return jnp.cos(angle), jnp.sin(angle)


def interpolate(child_block, theta_map, phi_map):
    lead_shape = child_block.shape[:3]
    grid_form = child_block.reshape(lead_shape + (THETA0, PHI0))
    along_theta = jnp.einsum('st,abctp->abcsp', theta_map, grid_form, precision=lax.Precision.HIGHEST)
    along_phi = jnp.einsum('abcsp,qp->abcsq', along_theta, phi_map, precision=lax.Precision.HIGHEST)
    return along_phi.reshape(lead_shape + (THETA1 * PHI1,))


def shift_phase(fine_grid, cos_table, sin_table):
    real_in = fine_grid[:, 0]
    imag_in = fine_grid[:, 1]
    cos_here = cos_table[:, None, :]
    sin_here = sin_table[:, None, :]
    real_out = real_in * cos_here - imag_in * sin_here
    imag_out = real_in * sin_here + imag_in * cos_here
    return jnp.stack([real_out, imag_out], axis=1)


def translate_terms(sources, table_rows, live_mask):
    real_part = sources[..., 0, :, :] * table_rows[..., 0, None, :] - sources[..., 1, :, :] * table_rows[..., 1, None, :]
    imag_part = sources[..., 0, :, :] * table_rows[..., 1, None, :] + sources[..., 1, :, :] * table_rows[..., 0, None, :]
    weight = live_mask[..., None, None]
    return jnp.stack([jnp.sum(weight * real_part, axis=-3), jnp.sum(weight * imag_part, axis=-3)], axis=-3)


def reference(patterns, translators, send_rows, far_slot, far_offset, far_count, children, octant):
    sender_base = (jnp.arange(N_BOX, dtype=jnp.int32) * BOX_DEV0)[:, None, None]
    source_global = jnp.transpose(send_rows + sender_base, (1, 0, 2)).reshape(N_BOX, N_BOX * SLOT)
    box_owner = jnp.arange(N_BOX * BOX_DEV0, dtype=jnp.int32) // BOX_DEV0
    far_global = jnp.take_along_axis(source_global[box_owner], far_slot, axis=1)

    def translate_box(box_args):
        rows_here, offsets_here, count_here = box_args
        live_mask = (jnp.arange(FAR, dtype=jnp.int32) < count_here).astype(jnp.float32)
        return translate_terms(patterns[rows_here], translators[offsets_here], live_mask)

    received = lax.map(translate_box, (far_global, far_offset, far_count))

    theta_map = theta_matrix(THETA1, THETA0)
    phi_map = phi_matrix(PHI1, PHI0)

    def aggregate_parent(member_rows):
        child_block = patterns[member_rows]
        fine_grid = interpolate(child_block, theta_map, phi_map)
        cos_table, sin_table = phase_tables(octant[member_rows])
        return jnp.sum(shift_phase(fine_grid, cos_table, sin_table), axis=0)

    upward = lax.map(aggregate_parent, children)
    return received, upward
```

```python
import functools

import jax
import jax.numpy as jnp
import numpy as np
from jax import lax
from jax.experimental import pallas as pl
from jax.experimental.pallas import tpu as pltpu
from jax.sharding import PartitionSpec as P

THETA0 = 64
PHI0 = 128
THETA1 = 128
PHI1 = 256
CH = 4
HALF_PHASE = 8.0
MESH = pl.DeviceIdType.MESH


def theta_matrix():
    fine = np.pi * (np.arange(THETA1) + 0.5) / THETA1
    coarse = np.pi * (np.arange(THETA0) + 0.5) / THETA0
    orders = np.arange(THETA0)
    weights = np.where(orders > 0, 2.0, 1.0)
    return (np.cos(fine[:, None] * orders) * weights) @ np.cos(coarse[:, None] * orders).T / THETA0


def phi_matrix():
    fine = 2.0 * np.pi * np.arange(PHI1) / PHI1
    coarse = 2.0 * np.pi * np.arange(PHI0) / PHI0
    orders = np.arange(PHI0 // 2 + 1)
    weights = np.where((orders == 0) | (orders == PHI0 // 2), 1.0, 2.0)
    delta = fine[:, None] - coarse[None, :]
    return np.sum(weights * np.cos(delta[:, :, None] * orders), axis=-1) / PHI0


def phase_tables():
    theta = np.pi * (np.arange(THETA1) + 0.5) / THETA1
    phi = 2.0 * np.pi * np.arange(PHI1) / PHI1
    ux = np.sin(theta)[:, None] * np.cos(phi)[None, :]
    uy = np.sin(theta)[:, None] * np.sin(phi)[None, :]
    uz = np.cos(theta)[:, None] * np.ones((1, PHI1))
    tables = []
    for o in range(4):
        sx, sy = 1.0 - 2.0 * (o % 2), 1.0 - 2.0 * (o // 2 % 2)
        angle = HALF_PHASE * (sx * ux + sy * uy + uz)
        tables.append(np.stack([np.cos(angle), np.sin(angle)]))
    return np.stack(tables).astype(np.float32)


def theta_blocks(n_dir):
    rows = THETA0 // n_dir
    m = theta_matrix().reshape(THETA1, n_dir, rows)
    out = np.zeros((2, THETA1, n_dir, 2, rows))
    for part in range(2):
        out[part, :, :, part, :] = m
    return out.reshape(2 * THETA1, n_dir * 2 * rows)


def halves(x):
    hi = jnp.asarray(x, jnp.float32).astype(jnp.bfloat16)
    lo = (jnp.asarray(x, jnp.float32) - hi.astype(jnp.float32)).astype(jnp.bfloat16)
    return hi, lo


def dot3(ah, al, bh, bl):
    dot = functools.partial(jnp.dot, preferred_element_type=jnp.float32)
    return dot(ah, bh) + (dot(al, bh) + dot(ah, bl))


def comm_kernel(
    n_box, n_dir, n_send, boxes, n_tr,
    send_ref, child_ref, oct_ref, pat_ref, ph_ref, pl_ref, mh_ref, ml_ref, tab_hbm, tr_hbm,
    src_out, up_out, tr_out,
    box_buf, dir_buf, dir_in, z_buf, up_buf, tab, tr, tc,
    box_send, box_recv, dir_send, dir_recv, up_send, up_recv, local_sem,
):
    box = lax.axis_index("box")
    here = lax.axis_index("dir")
    barrier = pltpu.get_barrier_semaphore()

    @pl.loop(1, n_dir)
    def _(i):
        pl.semaphore_signal(
            barrier, inc=1, device_id={"dir": lax.rem(here + i, n_dir)}, device_id_type=MESH
        )

    @pl.loop(1, n_box)
    def _(i):
        pl.semaphore_signal(
            barrier, inc=1, device_id={"box": lax.rem(box + i, n_box)}, device_id_type=MESH
        )

    tab_copy = pltpu.make_async_copy(tab_hbm, tab, local_sem.at[0])
    tr_copy = pltpu.make_async_copy(tr_hbm, tr, local_sem.at[1])
    tr_copy.start()
    tab_copy.start()


    @pl.loop(0, n_dir)
    def _(r):
        for c in range(CH):
            dir_buf[r, c] = pat_ref[lax.rem(child_ref[c, r], boxes)]

    for c in range(CH):
        dir_in[here, c] = pat_ref[lax.rem(child_ref[c, here], boxes)]

    @pl.loop(0, n_box)
    def _(r):
        for j in range(n_send):
            box_buf[r, j] = pat_ref[send_ref[j, 0, r]]

    pl.semaphore_wait(barrier, n_dir + n_box - 2)

    def dir_copy(i):
        to = lax.rem(here + i, n_dir)
        return pltpu.make_async_remote_copy(
            src_ref=dir_buf.at[to], dst_ref=dir_in.at[here],
            send_sem=dir_send.at[i], recv_sem=dir_recv.at[i],
            device_id={"dir": to}, device_id_type=MESH,
        )

    def box_copy(i):
        to = lax.rem(box + i, n_box)
        return pltpu.make_async_remote_copy(
            src_ref=box_buf.at[to], dst_ref=src_out.at[box],
            send_sem=box_send.at[i], recv_sem=box_recv.at[i],
            device_id={"box": to}, device_id_type=MESH,
        )

    def up_copy(i):
        to = lax.rem(here + i, n_dir)
        return pltpu.make_async_remote_copy(
            src_ref=up_buf.at[to], dst_ref=up_out.at[here],
            send_sem=up_send.at[i], recv_sem=up_recv.at[i],
            device_id={"dir": to}, device_id_type=MESH,
        )

    @pl.loop(1, n_dir)
    def _(i):
        dir_copy(i).start()

    @pl.loop(1, n_box)
    def _(i):
        box_copy(i).start()

    own_box = pltpu.make_async_copy(box_buf.at[box], src_out.at[box], local_sem.at[2])
    own_box.start()

    tr_copy.wait()
    low = lax.broadcasted_iota(jnp.int32, (8, 128), 0) < 4

    @pl.loop(0, n_tr // 2)
    def _(k):
        at = pl.multiple_of(k * 16, 16)
        re = tr[pl.ds(at, 8, stride=2), :]
        im = tr[pl.ds(at + 1, 8, stride=2), :]
        tc[2 * k] = jnp.where(low, re, pltpu.roll(im, 4, 0))
        tc[2 * k + 1] = jnp.where(low, pltpu.roll(re, 4, 0), im)

    tc[n_tr] = jnp.zeros((8, 128), jnp.float32)
    tc_copy = pltpu.make_async_copy(tc, tr_out, local_sem.at[3])

    @pl.loop(1, n_dir)
    def _(i):
        dir_copy(i).wait_recv()

    tc_copy.start()

    for c in range(CH):
        x = dir_in[:, c].reshape(n_dir * 8, 128)
        y = dot3(*halves(x), ph_ref[...], pl_ref[...])
        z_buf[c] = dot3(mh_ref[...], ml_ref[...], *halves(y))

    tab_copy.wait()
    octants = [oct_ref[lax.rem(child_ref[c, here], boxes)] for c in range(CH)]
    table = [jnp.where(o < 4, o, 7 - o) for o in octants]
    sign = [jnp.where(o < 4, 1.0, -1.0).astype(jnp.float32) for o in octants]

    @pl.loop(0, n_dir)
    def _(r):
        at = pl.multiple_of(r * 8, 8)
        for half in range(2):
            cols = pl.ds(half * 128, 128)
            re = im = None
            for c in range(CH):
                zr = z_buf[c, pl.ds(at, 8), cols]
                zi = z_buf[c, pl.ds(at + THETA1, 8), cols]
                cos = tab[table[c], 0, pl.ds(at, 8), cols]
                sin = tab[table[c], 1, pl.ds(at, 8), cols] * sign[c]
                a, b = zr * cos - zi * sin, zr * sin + zi * cos
                re, im = (a, b) if c == 0 else (re + a, im + b)
            up_buf[r, 0, pl.ds(half, 8, stride=2), :] = re
            up_buf[r, 1, pl.ds(half, 8, stride=2), :] = im

    @pl.loop(1, n_dir)
    def _(i):
        up_copy(i).start()

    own_up = pltpu.make_async_copy(up_buf.at[here], up_out.at[here], local_sem.at[4])
    own_up.start()

    @pl.loop(1, n_dir)
    def _(i):
        dir_copy(i).wait_send()

    own_box.wait()
    tc_copy.wait()
    own_up.wait()

    @pl.loop(1, n_dir)
    def _(i):
        up_copy(i).wait()

    @pl.loop(1, n_box)
    def _(i):
        box_copy(i).wait()


def far_kernel(n_far, boxes, n_tr, slot_ref, off_ref, cnt_ref, src_ref, tr_ref, up_ref, out_ref, up_out):
    up_out[...] = up_ref[...]
    low = lax.broadcasted_iota(jnp.int32, (8, 128), 0) < 4

    @pl.loop(0, boxes)
    def _(b):
        count = cnt_ref[b]
        p, q = [None, None], [None, None]
        for f in range(n_far):
            t = tr_ref[jnp.where(f < count, off_ref[f, b], n_tr)]
            a = src_ref[slot_ref[f, b]]
            u, v = a * t, pltpu.roll(a, 4, 0) * t
            k = f % 2
            p[k], q[k] = (u, v) if f < 2 else (p[k] + u, q[k] + v)
        p, q = p[0] + p[1], q[0] + q[1]
        out_ref[b] = jnp.where(low, p - pltpu.roll(p, 4, 0), q + pltpu.roll(q, 4, 0))


def shards(patterns, translators, send_rows, far_slot, far_offset, far_count, children, octant):
    n_box, n_dir = lax.axis_size("box"), lax.axis_size("dir")
    boxes, n_send = patterns.shape[0], send_rows.shape[2]
    n_tr, n_far = translators.shape[0], far_slot.shape[1]
    pat = patterns.reshape(boxes, 8, 128)
    tr = translators.reshape(n_tr, 2, 4, 128).transpose(0, 2, 1, 3).reshape(n_tr * 8, 128)
    ph, plo = halves(phi_matrix().T)
    mh, mlo = halves(theta_blocks(n_dir))
    vmem, smem = pl.BlockSpec(memory_space=pltpu.VMEM), pl.BlockSpec(memory_space=pltpu.SMEM)
    hbm, anywhere = pl.BlockSpec(memory_space=pltpu.HBM), pl.BlockSpec(memory_space=pl.ANY)
    f32 = jnp.float32
    dma = pltpu.SemaphoreType.DMA
    src, up, tc = pl.pallas_call(
        functools.partial(comm_kernel, n_box, n_dir, n_send, boxes, n_tr),
        out_shape=(
            jax.ShapeDtypeStruct((n_box, n_send, 8, 128), f32),
            jax.ShapeDtypeStruct((n_dir, 2, 16, 128), f32),
            jax.ShapeDtypeStruct((n_tr + 1, 8, 128), f32),
        ),
        in_specs=[smem] * 3 + [vmem] * 5 + [hbm] * 2,
        out_specs=(anywhere, anywhere, anywhere),
        scratch_shapes=[
            pltpu.VMEM((n_box, n_send, 8, 128), f32),
            pltpu.VMEM((n_dir, CH, 8, 128), f32),
            pltpu.VMEM((n_dir, CH, 8, 128), f32),
            pltpu.VMEM((CH, 2 * THETA1, PHI1), f32),
            pltpu.VMEM((n_dir, 2, 16, 128), f32),
            pltpu.VMEM((4, 2, THETA1, PHI1), f32),
            pltpu.VMEM((n_tr * 8, 128), f32),
            pltpu.VMEM((n_tr + 1, 8, 128), f32),
            dma((n_box,)), dma((n_box,)),
            dma((n_dir,)), dma((n_dir,)),
            dma((n_dir,)), dma((n_dir,)),
            dma((5,)),
        ],
        compiler_params=pltpu.CompilerParams(
            collective_id=0, has_side_effects=True, vmem_limit_bytes=16 << 20
        ),
        name="exchange",
    )(send_rows.transpose(2, 0, 1), children.T, octant, pat, ph, plo, mh, mlo, jnp.asarray(phase_tables()), tr)
    received, upward = pl.pallas_call(
        functools.partial(far_kernel, n_far, boxes, n_tr),
        out_shape=(
            jax.ShapeDtypeStruct((boxes, 8, 128), f32),
            jax.ShapeDtypeStruct((n_dir, 2, 16, 128), f32),
        ),
        in_specs=[smem] * 3 + [vmem] * 3,
        out_specs=(vmem, vmem),
        compiler_params=pltpu.CompilerParams(vmem_limit_bytes=16 << 20),
        name="far",
    )(far_slot.T, far_offset.T, far_count, src.reshape(n_box * n_send, 8, 128), tc, up)
    return received.reshape(patterns.shape), upward.reshape(children.shape[0], 2, 1, -1)


def solution(mesh):
    return jax.shard_map(
        shards,
        mesh=mesh,
        in_specs=(
            P("box", None, None, "dir"),
            P(None, None, "dir"),
            P("box", None, None),
            P("box", None),
            P("box", None),
            P("box"),
            P("box", None),
            P("box"),
        ),
        out_specs=(P("box", None, None, "dir"), P("box", None, None, "dir")),
        check_vma=False,
    )
```

```python
import functools

import jax
import jax.numpy as jnp
import numpy as np
from jax import lax
from jax.experimental import pallas as pl
from jax.experimental.pallas import tpu as pltpu
from jax.sharding import PartitionSpec as P

THETA0 = 64
PHI0 = 128
THETA1 = 128
PHI1 = 256
CH = 4
HALF_PHASE = 8.0
MESH = pl.DeviceIdType.MESH
PIECE = 16


def theta_matrix():
    fine = np.pi * (np.arange(THETA1) + 0.5) / THETA1
    coarse = np.pi * (np.arange(THETA0) + 0.5) / THETA0
    orders = np.arange(THETA0)
    weights = np.where(orders > 0, 2.0, 1.0)
    return (np.cos(fine[:, None] * orders) * weights) @ np.cos(coarse[:, None] * orders).T / THETA0


def phi_matrix():
    fine = 2.0 * np.pi * np.arange(PHI1) / PHI1
    coarse = 2.0 * np.pi * np.arange(PHI0) / PHI0
    orders = np.arange(PHI0 // 2 + 1)
    weights = np.where((orders == 0) | (orders == PHI0 // 2), 1.0, 2.0)
    delta = fine[:, None] - coarse[None, :]
    return np.sum(weights * np.cos(delta[:, :, None] * orders), axis=-1) / PHI0


def phase_tables():
    theta = np.pi * (np.arange(THETA1) + 0.5) / THETA1
    phi = 2.0 * np.pi * np.arange(PHI1) / PHI1
    ux = np.sin(theta)[:, None] * np.cos(phi)[None, :]
    uy = np.sin(theta)[:, None] * np.sin(phi)[None, :]
    uz = np.cos(theta)[:, None] * np.ones((1, PHI1))
    tables = []
    for o in range(4):
        sx, sy = 1.0 - 2.0 * (o % 2), 1.0 - 2.0 * (o // 2 % 2)
        angle = HALF_PHASE * (sx * ux + sy * uy + uz)
        tables.append(np.stack([np.cos(angle), np.sin(angle)]))
    return np.stack(tables).astype(np.float32)


def theta_blocks(n_dir):
    rows = THETA0 // n_dir
    m = theta_matrix().reshape(THETA1, n_dir, rows)
    out = np.zeros((2, THETA1, n_dir, 2, rows))
    for part in range(2):
        out[part, :, :, part, :] = m
    return out.reshape(2 * THETA1, n_dir * 2 * rows)


def halves(x):
    hi = jnp.asarray(x, jnp.float32).astype(jnp.bfloat16)
    lo = (jnp.asarray(x, jnp.float32) - hi.astype(jnp.float32)).astype(jnp.bfloat16)
    return hi, lo


def dot3(ah, al, bh, bl):
    dot = functools.partial(jnp.dot, preferred_element_type=jnp.float32)
    return dot(ah, bh) + (dot(al, bh) + dot(ah, bl))


def kernel(
    n_box, n_dir, n_send, boxes, n_tr, n_far,
    send_hbm, child_hbm, oct_hbm, slot_hbm, off_hbm, cnt_hbm, pat_hbm, ph_hbm, pl_hbm, mh_hbm, ml_hbm, tab_hbm, tr_hbm,
    src, tc, row_s, row_t, up_out,
    send_ref, child_ref, oct_ref, pat, ph, plo, mh, mlo, tab, tr, slot, off, cnt,
    box_buf, dir_buf, dir_in, z_buf, up_buf,
    box_send, box_recv, dir_send, dir_recv, up_send, up_recv, sem,
):
    box = lax.axis_index("box")
    here = lax.axis_index("dir")
    rows = 8 * n_send
    barrier = pltpu.get_barrier_semaphore()

    def local(k, source, target):
        copy = pltpu.make_async_copy(source, target, sem.at[k])
        copy.start()
        return copy

    first = [
        local(0, child_hbm, child_ref), local(1, pat_hbm, pat), local(2, send_hbm, send_ref),
    ]

    levels, lines = n_box // 4, n_dir // 2
    level = [lax.rem(box // 4 + k, levels) * 4 for k in range(levels)]
    spot = [lax.rem(lax.rem(box, 4) + k, 4) for k in range(4)]
    side = [lax.rem(here // lines + k, 2) * lines for k in range(2)]
    line = [lax.rem(lax.rem(here, lines) + k, lines) for k in range(lines)]

    def rounds(n):
        return sorted(range(n), key=lambda k: (-min(k, n - k), k))

    box_peers = [(4 * k + j, level[k] + spot[j]) for k in rounds(levels) for j in range(4) if k + j]
    dir_peers = [(lines * j + k, side[j] + line[k]) for k in rounds(lines) for j in range(2) if k + j]

    def greet(axis, to):
        pl.semaphore_signal(barrier, inc=1, device_id={axis: to}, device_id_type=MESH)

    for _, to in box_peers:
        greet("box", to)
    for _, to in dir_peers:
        greet("dir", to)

    later = [
        local(3, oct_hbm, oct_ref), local(4, ph_hbm, ph), local(5, pl_hbm, plo), local(6, mh_hbm, mh),
        local(7, ml_hbm, mlo), local(8, tab_hbm, tab),
    ]
    tables = [
        local(9, tr_hbm, tr), local(10, slot_hbm, slot), local(11, off_hbm, off), local(12, cnt_hbm, cnt),
    ]

    for copy in first:
        copy.wait()

    def child(c, r):
        return lax.rem(child_ref[c, r], boxes)

    @pl.loop(0, n_dir // 4)
    def _(k):
        for r in range(4):
            for c in range(CH):
                dir_buf[4 * k + r, c] = pat[child(c, 4 * k + r)]

    for c in range(CH):
        dir_in[here, c] = pat[child(c, here)]

    @pl.loop(0, n_box // 4)
    def _(k):
        for r in range(4):
            for j in range(n_send):
                at = pl.multiple_of((4 * k + r) * rows + j * 8, 8)
                box_buf[pl.ds(at, 8), :] = pat[send_ref[j, 0, 4 * k + r]]

    for j in range(n_send):
        src[pl.ds(pl.multiple_of(box * rows + j * 8, 8), 8), :] = pat[send_ref[j, 0, box]]

    pl.semaphore_wait(barrier, n_dir + n_box - 2)

    def dir_copy(i, to):
        return pltpu.make_async_remote_copy(
            src_ref=dir_buf.at[to], dst_ref=dir_in.at[here],
            send_sem=dir_send.at[i], recv_sem=dir_recv.at[i],
            device_id={"dir": to}, device_id_type=MESH,
        )

    def box_copy(i, to):
        return pltpu.make_async_remote_copy(
            src_ref=box_buf.at[pl.ds(pl.multiple_of(to * rows, 8), rows)],
            dst_ref=src.at[pl.ds(pl.multiple_of(box * rows, 8), rows)],
            send_sem=box_send.at[i], recv_sem=box_recv.at[i],
            device_id={"box": to}, device_id_type=MESH,
        )

    def up_copy(i, to):
        return pltpu.make_async_remote_copy(
            src_ref=up_buf.at[to], dst_ref=up_out.at[here],
            send_sem=up_send.at[i], recv_sem=up_recv.at[i],
            device_id={"dir": to}, device_id_type=MESH,
        )

    for peer in dir_peers:
        dir_copy(*peer).start()

    for peer in box_peers:
        box_copy(*peer).start()

    for copy in tables:
        copy.wait()
    low = lax.broadcasted_iota(jnp.int32, (8, 128), 0) < 4

    @pl.loop(0, n_tr // 2)
    def _(k):
        at = pl.multiple_of(k * 16, 16)
        re = tr[pl.ds(at, 8, stride=2), :]
        im = tr[pl.ds(at + 1, 8, stride=2), :]
        tc[pl.ds(at, 8), :] = jnp.where(low, re, pltpu.roll(im, 4, 0))
        tc[pl.ds(at + 8, 8), :] = jnp.where(low, pltpu.roll(re, 4, 0), im)

    tc[pl.ds(n_tr * 8, 8), :] = jnp.zeros((8, 128), jnp.float32)

    live = lax.broadcasted_iota(jnp.int32, (n_far, boxes), 0) < cnt[...]
    row_s[...] = slot[...] * 8
    row_t[...] = jnp.where(live, off[...], n_tr) * 8

    @pl.loop(1, n_dir)
    def _(i):
        dir_copy(i, here).wait_recv()

    for copy in later:
        copy.wait()

    for c in range(CH):
        x = dir_in[:, c].reshape(n_dir * 8, 128)
        y = dot3(*halves(x), ph[...], plo[...])
        z_buf[c] = dot3(mh[...], mlo[...], *halves(y))

    octants = [oct_ref[child(c, here)] for c in range(CH)]
    table = [jnp.where(o < 4, o, 7 - o) for o in octants]
    sign = [jnp.where(o < 4, 1.0, -1.0).astype(jnp.float32) for o in octants]

    @pl.loop(0, n_dir)
    def _(r):
        at = pl.multiple_of(r * 8, 8)
        for half in range(2):
            cols = pl.ds(half * 128, 128)
            re = im = None
            for c in range(CH):
                zr = z_buf[c, pl.ds(at, 8), cols]
                zi = z_buf[c, pl.ds(at + THETA1, 8), cols]
                cos = tab[table[c], 0, pl.ds(at, 8), cols]
                sin = tab[table[c], 1, pl.ds(at, 8), cols] * sign[c]
                a, b = zr * cos - zi * sin, zr * sin + zi * cos
                re, im = (a, b) if c == 0 else (re + a, im + b)
            up_buf[r, 0, pl.ds(half, 8, stride=2), :] = re
            up_buf[r, 1, pl.ds(half, 8, stride=2), :] = im

    for peer in dir_peers:
        up_copy(*peer).start()

    own_up = local(14, up_buf.at[here], up_out.at[here])

    @pl.loop(1, n_dir)
    def _(i):
        dir_copy(i, here).wait_send()

    own_up.wait()


    @pl.loop(1, n_box)
    def _(i):
        box_copy(i, box).wait_recv()

    @pl.loop(1, n_dir)
    def _(i):
        up_copy(i, here).wait()

    @pl.loop(1, n_box)
    def _(i):
        box_copy(i, box).wait_send()


def far_kernel(n_far, boxes, row_s, row_t, src, tc, up, far_out, up_out, held, sem):
    up_copy = pltpu.make_async_copy(up, up_out, sem.at[0])
    up_copy.start()
    low = lax.broadcasted_iota(jnp.int32, (8, 128), 0) < 4
    copies = []
    for b in range(boxes):
        p, q = [None, None], [None, None]
        for f in range(n_far):
            t = tc[pl.ds(pl.multiple_of(row_t[f, b], 8), 8), :]
            a = src[pl.ds(pl.multiple_of(row_s[f, b], 8), 8), :]
            u, v = a * t, pltpu.roll(a, 4, 0) * t
            k = f % 2
            p[k], q[k] = (u, v) if f < 2 else (p[k] + u, q[k] + v)
        p, q = p[0] + p[1], q[0] + q[1]
        held[b] = jnp.where(low, p - pltpu.roll(p, 4, 0), q + pltpu.roll(q, 4, 0))
        if b % PIECE == PIECE - 1:
            part = pl.ds(b + 1 - PIECE, PIECE)
            copies.append(pltpu.make_async_copy(held.at[part], far_out.at[part], sem.at[1 + b // PIECE]))
            copies[-1].start()
    for copy in [up_copy] + copies:
        copy.wait()


def shards(patterns, translators, send_rows, far_slot, far_offset, far_count, children, octant):
    n_box, n_dir = lax.axis_size("box"), lax.axis_size("dir")
    boxes, n_send = patterns.shape[0], send_rows.shape[2]
    n_tr, n_far = translators.shape[0], far_slot.shape[1]
    pat = patterns.reshape(boxes, 8, 128)
    tr = translators.reshape(n_tr, 2, 4, 128).transpose(0, 2, 1, 3).reshape(n_tr * 8, 128)
    vmem, smem = pl.BlockSpec(memory_space=pltpu.VMEM), pl.BlockSpec(memory_space=pltpu.SMEM)
    hbm = pl.BlockSpec(memory_space=pltpu.HBM)
    f32, i32, bf16 = jnp.float32, jnp.int32, jnp.bfloat16
    dma = pltpu.SemaphoreType.DMA
    operands = (
        send_rows.transpose(2, 0, 1), children.T, octant, far_slot.T, far_offset.T, far_count.reshape(1, boxes),
        pat, *halves(phi_matrix().T), *halves(theta_blocks(n_dir)), jnp.asarray(phase_tables()), tr,
    )
    received_shape = jax.ShapeDtypeStruct((boxes, 8, 128), f32)
    upward_shape = jax.ShapeDtypeStruct((n_dir, 2, 16, 128), f32)
    row_shape = jax.ShapeDtypeStruct((n_far, boxes), i32)
    src, tc, row_s, row_t, upward = pl.pallas_call(
        functools.partial(kernel, n_box, n_dir, n_send, boxes, n_tr, n_far),
        out_shape=(
            jax.ShapeDtypeStruct((n_box * n_send * 8, 128), f32),
            jax.ShapeDtypeStruct((n_tr * 8 + 8, 128), f32),
            row_shape, row_shape, upward_shape,
        ),
        in_specs=[hbm] * len(operands),
        out_specs=(vmem,) * 5,
        scratch_shapes=[
            pltpu.SMEM((n_send, 1, n_box), i32), pltpu.SMEM((CH, n_dir), i32), pltpu.SMEM((boxes,), i32),
            pltpu.VMEM((boxes, 8, 128), f32),
            pltpu.VMEM((PHI0, PHI1), bf16), pltpu.VMEM((PHI0, PHI1), bf16),
            pltpu.VMEM((2 * THETA1, 128), bf16), pltpu.VMEM((2 * THETA1, 128), bf16),
            pltpu.VMEM((4, 2, THETA1, PHI1), f32),
            pltpu.VMEM((n_tr * 8, 128), f32),
            pltpu.VMEM((n_far, boxes), i32), pltpu.VMEM((n_far, boxes), i32), pltpu.VMEM((1, boxes), i32),
            pltpu.VMEM((n_box * n_send * 8, 128), f32),
            pltpu.VMEM((n_dir, CH, 8, 128), f32),
            pltpu.VMEM((n_dir, CH, 8, 128), f32),
            pltpu.VMEM((CH, 2 * THETA1, PHI1), f32),
            pltpu.VMEM((n_dir, 2, 16, 128), f32),
            dma((n_box,)), dma((n_box,)),
            dma((n_dir,)), dma((n_dir,)),
            dma((n_dir,)), dma((n_dir,)),
            dma((15,)),
        ],
        compiler_params=pltpu.CompilerParams(
            collective_id=0, has_side_effects=True, vmem_limit_bytes=24 << 20
        ),
        name="exchange",
    )(*(pltpu.with_memory_space_constraint(x, pltpu.HBM) for x in operands))
    received, upward = pl.pallas_call(
        functools.partial(far_kernel, n_far, boxes),
        out_shape=(received_shape, upward_shape),
        in_specs=[smem, smem, vmem, vmem, vmem],
        out_specs=(hbm, hbm),
        scratch_shapes=[pltpu.VMEM((boxes, 8, 128), f32), dma((1 + boxes // PIECE,))],
        compiler_params=pltpu.CompilerParams(vmem_limit_bytes=8 << 20),
        name="far",
    )(row_s, row_t, src, tc, upward)
    return received.reshape(patterns.shape), upward.reshape(children.shape[0], 2, 1, -1)


def solution(mesh):
    return jax.shard_map(
        shards,
        mesh=mesh,
        in_specs=(
            P("box", None, None, "dir"),
            P(None, None, "dir"),
            P("box", None, None),
            P("box", None),
            P("box", None),
            P("box"),
            P("box", None),
            P("box"),
        ),
        out_specs=(P("box", None, None, "dir"), P("box", None, None, "dir")),
        check_vma=False,
    )
```

```python
import functools

import jax
import jax.numpy as jnp
import numpy as np
from jax import lax
from jax.experimental import pallas as pl
from jax.experimental.pallas import tpu as pltpu
from jax.sharding import PartitionSpec as P

THETA0 = 64
PHI0 = 128
THETA1 = 128
PHI1 = 256
CH = 4
HALF_PHASE = 8.0
MESH = pl.DeviceIdType.MESH
PIECE = 16


def theta_matrix():
    fine = np.pi * (np.arange(THETA1) + 0.5) / THETA1
    coarse = np.pi * (np.arange(THETA0) + 0.5) / THETA0
    orders = np.arange(THETA0)
    weights = np.where(orders > 0, 2.0, 1.0)
    return (np.cos(fine[:, None] * orders) * weights) @ np.cos(coarse[:, None] * orders).T / THETA0


def phi_matrix():
    fine = 2.0 * np.pi * np.arange(PHI1) / PHI1
    coarse = 2.0 * np.pi * np.arange(PHI0) / PHI0
    orders = np.arange(PHI0 // 2 + 1)
    weights = np.where((orders == 0) | (orders == PHI0 // 2), 1.0, 2.0)
    delta = fine[:, None] - coarse[None, :]
    return np.sum(weights * np.cos(delta[:, :, None] * orders), axis=-1) / PHI0


def phase_tables():
    theta = np.pi * (np.arange(THETA1) + 0.5) / THETA1
    phi = 2.0 * np.pi * np.arange(PHI1) / PHI1
    ux = np.sin(theta)[:, None] * np.cos(phi)[None, :]
    uy = np.sin(theta)[:, None] * np.sin(phi)[None, :]
    uz = np.cos(theta)[:, None] * np.ones((1, PHI1))
    tables = []
    for o in range(4):
        sx, sy = 1.0 - 2.0 * (o % 2), 1.0 - 2.0 * (o // 2 % 2)
        angle = HALF_PHASE * (sx * ux + sy * uy + uz)
        tables.append(np.stack([np.cos(angle), np.sin(angle)]))
    return np.stack(tables).astype(np.float32)


def theta_blocks(n_dir):
    rows = THETA0 // n_dir
    m = theta_matrix().reshape(THETA1, n_dir, rows)
    out = np.zeros((2, THETA1, n_dir, 2, rows))
    for part in range(2):
        out[part, :, :, part, :] = m
    return out.reshape(2 * THETA1, n_dir * 2 * rows)


def halves(x):
    hi = jnp.asarray(x, jnp.float32).astype(jnp.bfloat16)
    lo = (jnp.asarray(x, jnp.float32) - hi.astype(jnp.float32)).astype(jnp.bfloat16)
    return hi, lo


def dot3(ah, al, bh, bl):
    dot = functools.partial(jnp.dot, preferred_element_type=jnp.float32)
    return dot(ah, bh) + (dot(al, bh) + dot(ah, bl))


def kernel(
    n_box, n_dir, n_send, boxes, n_tr, n_far,
    send_hbm, child_hbm, oct_hbm, slot_hbm, off_hbm, cnt_hbm, pat_hbm, ph_hbm, pl_hbm, mh_hbm, ml_hbm, tab_hbm, tr_hbm,
    src, tc, row_s, row_t, up_out,
    send_ref, child_ref, oct_ref, pat, ph, plo, mh, mlo, tab, tr, slot, off, cnt,
    box_buf, dir_buf, dir_in, z_buf, up_buf,
    box_send, box_recv, dir_send, dir_recv, up_send, up_recv, sem,
):
    box = lax.axis_index("box")
    here = lax.axis_index("dir")
    rows = 8 * n_send
    barrier = pltpu.get_barrier_semaphore()

    def local(k, source, target):
        copy = pltpu.make_async_copy(source, target, sem.at[k])
        copy.start()
        return copy

    first = [
        local(0, send_hbm, send_ref), local(1, pat_hbm, pat), local(2, child_hbm, child_ref),
    ]

    levels, lines = n_box // 4, n_dir // 2
    level, spot = box // 4, lax.rem(box, 4)
    side, line = here // lines, lax.rem(here, lines)
    spots = [lax.rem(spot + j, 4) for j in range(4)]
    sides = [lax.rem(side + j, 2) * lines for j in range(2)]

    def far_first(k, n):
        return n // 2 + (1 - 2 * lax.rem(k, 2)) * ((k + 1) // 2)

    def each_box(visit):
        @pl.loop(0, levels - 1)
        def _(k):
            step = far_first(k, levels)
            at = lax.rem(level + step, levels) * 4
            for j in (2, 3, 1, 0):
                visit(at + spots[j])

        for j in (2, 3, 1):
            visit(level * 4 + spots[j])

    def each_dir(visit):
        @pl.loop(0, lines - 1)
        def _(k):
            step = far_first(k, lines)
            at = lax.rem(line + step, lines)
            for j in (1, 0):
                visit(sides[j] + at)

        visit(sides[1] + line)

    def greet(axis, to):
        pl.semaphore_signal(barrier, inc=1, device_id={axis: to}, device_id_type=MESH)

    each_box(lambda to: greet("box", to))
    each_dir(lambda to: greet("dir", to))

    for copy in first:
        copy.wait()

    @pl.loop(0, n_box // 4)
    def _(k):
        for r in range(4):
            for j in range(n_send):
                at = pl.multiple_of((4 * k + r) * rows + j * 8, 8)
                box_buf[pl.ds(at, 8), :] = pat[send_ref[j, 0, 4 * k + r]]

    def child(c, r):
        return jnp.maximum(child_ref[c, r] - box * boxes, 0)

    @pl.loop(0, n_dir // 2)
    def _(k):
        for r in range(2):
            for c in range(CH):
                dir_buf[2 * k + r, c] = pat[child(c, 2 * k + r)]

    pl.semaphore_wait(barrier, n_dir + n_box - 2)

    def dir_copy(to):
        return pltpu.make_async_remote_copy(
            src_ref=dir_buf.at[to], dst_ref=dir_in.at[here],
            send_sem=dir_send.at[0], recv_sem=dir_recv.at[0],
            device_id={"dir": to}, device_id_type=MESH,
        )

    def box_copy(to):
        return pltpu.make_async_remote_copy(
            src_ref=box_buf.at[pl.ds(pl.multiple_of(to * rows, 8), rows)],
            dst_ref=src.at[pl.ds(pl.multiple_of(box * rows, 8), rows)],
            send_sem=box_send.at[0], recv_sem=box_recv.at[0],
            device_id={"box": to}, device_id_type=MESH,
        )

    def up_copy(to):
        return pltpu.make_async_remote_copy(
            src_ref=up_buf.at[to], dst_ref=up_out.at[here],
            send_sem=up_send.at[0], recv_sem=up_recv.at[0],
            device_id={"dir": to}, device_id_type=MESH,
        )

    each_dir(lambda to: dir_copy(to).start())

    each_box(lambda to: box_copy(to).start())

    def all_of(source, target, send_sem, recv_sem):
        return pltpu.make_async_remote_copy(
            src_ref=source, dst_ref=target, send_sem=send_sem.at[0], recv_sem=recv_sem.at[0],
            device_id={"box": lax.rem(box + 1, n_box)}, device_id_type=MESH,
        )

    all_dir = all_of(
        dir_buf.at[pl.ds(0, n_dir - 1)], dir_in.at[pl.ds(0, n_dir - 1)], dir_send, dir_recv
    )
    all_up = all_of(up_buf.at[pl.ds(0, n_dir - 1)], up_out.at[pl.ds(0, n_dir - 1)], up_send, up_recv)
    all_box = all_of(
        box_buf.at[pl.ds(0, (n_box - 1) * rows)], src.at[pl.ds(0, (n_box - 1) * rows)], box_send, box_recv
    )

    for c in range(CH):
        dir_in[here, c] = pat[child(c, here)]

    for j in range(n_send):
        src[pl.ds(pl.multiple_of(box * rows + j * 8, 8), 8), :] = pat[send_ref[j, 0, box]]

    later = [
        local(3, oct_hbm, oct_ref), local(4, ph_hbm, ph), local(5, pl_hbm, plo), local(6, mh_hbm, mh),
        local(7, ml_hbm, mlo), local(8, tab_hbm, tab),
    ]
    tables = [
        local(9, tr_hbm, tr), local(10, slot_hbm, slot), local(11, off_hbm, off), local(12, cnt_hbm, cnt),
    ]

    for copy in tables:
        copy.wait()
    low = lax.broadcasted_iota(jnp.int32, (8, 128), 0) < 4

    @pl.loop(0, n_tr // 2)
    def _(k):
        at = pl.multiple_of(k * 16, 16)
        re = tr[pl.ds(at, 8, stride=2), :]
        im = tr[pl.ds(at + 1, 8, stride=2), :]
        tc[pl.ds(at, 8), :] = jnp.where(low, re, pltpu.roll(im, 4, 0))
        tc[pl.ds(at + 8, 8), :] = jnp.where(low, pltpu.roll(re, 4, 0), im)

    tc[pl.ds(n_tr * 8, 8), :] = jnp.zeros((8, 128), jnp.float32)

    live = lax.broadcasted_iota(jnp.int32, (n_far, boxes), 0) < cnt[...]
    row_s[...] = slot[...] * 8
    row_t[...] = jnp.where(live, off[...], n_tr) * 8

    all_dir.wait_recv()

    for copy in later:
        copy.wait()

    for c in range(CH):
        x = dir_in[:, c].reshape(n_dir * 8, 128)
        y = dot3(*halves(x), ph[...], plo[...])
        z_buf[c] = dot3(mh[...], mlo[...], *halves(y))

    octants = [oct_ref[child(c, here)] for c in range(CH)]
    table = [jnp.where(o < 4, o, 7 - o) for o in octants]
    sign = [jnp.where(o < 4, 1.0, -1.0).astype(jnp.float32) for o in octants]

    @pl.loop(0, n_dir)
    def _(r):
        at = pl.multiple_of(r * 8, 8)
        for half in range(2):
            cols = pl.ds(half * 128, 128)
            re = im = None
            for c in range(CH):
                zr = z_buf[c, pl.ds(at, 8), cols]
                zi = z_buf[c, pl.ds(at + THETA1, 8), cols]
                cos = tab[table[c], 0, pl.ds(at, 8), cols]
                sin = tab[table[c], 1, pl.ds(at, 8), cols] * sign[c]
                a, b = zr * cos - zi * sin, zr * sin + zi * cos
                re, im = (a, b) if c == 0 else (re + a, im + b)
            up_buf[r, 0, pl.ds(half, 8, stride=2), :] = re
            up_buf[r, 1, pl.ds(half, 8, stride=2), :] = im

    each_dir(lambda to: up_copy(to).start())

    own_up = local(14, up_buf.at[here], up_out.at[here])

    all_dir.wait_send()

    own_up.wait()


    all_box.wait_recv()

    all_up.wait()

    all_box.wait_send()


def far_kernel(n_far, boxes, row_s, row_t, src, tc, up, far_out, up_out, held, sem):
    up_copy = pltpu.make_async_copy(up, up_out, sem.at[0])
    up_copy.start()
    low = lax.broadcasted_iota(jnp.int32, (8, 128), 0) < 4
    copies = []
    for b in range(boxes):
        p, q = [None, None], [None, None]
        for f in range(n_far):
            t = tc[pl.ds(pl.multiple_of(row_t[f, b], 8), 8), :]
            a = src[pl.ds(pl.multiple_of(row_s[f, b], 8), 8), :]
            u, v = a * t, pltpu.roll(a, 4, 0) * t
            k = f % 2
            p[k], q[k] = (u, v) if f < 2 else (p[k] + u, q[k] + v)
        p, q = p[0] + p[1], q[0] + q[1]
        held[b] = jnp.where(low, p - pltpu.roll(p, 4, 0), q + pltpu.roll(q, 4, 0))
        if b % PIECE == PIECE - 1:
            part = pl.ds(b + 1 - PIECE, PIECE)
            copies.append(pltpu.make_async_copy(held.at[part], far_out.at[part], sem.at[1 + b // PIECE]))
            copies[-1].start()
    for copy in [up_copy] + copies:
        copy.wait()


def shards(patterns, translators, send_rows, far_slot, far_offset, far_count, children, octant):
    n_box, n_dir = lax.axis_size("box"), lax.axis_size("dir")
    boxes, n_send = patterns.shape[0], send_rows.shape[2]
    n_tr, n_far = translators.shape[0], far_slot.shape[1]
    pat = patterns.reshape(boxes, 8, 128)
    tr = translators.reshape(n_tr, 2, 4, 128).transpose(0, 2, 1, 3).reshape(n_tr * 8, 128)
    vmem, smem = pl.BlockSpec(memory_space=pltpu.VMEM), pl.BlockSpec(memory_space=pltpu.SMEM)
    hbm = pl.BlockSpec(memory_space=pltpu.HBM)
    f32, i32, bf16 = jnp.float32, jnp.int32, jnp.bfloat16
    dma = pltpu.SemaphoreType.DMA
    operands = (
        send_rows.transpose(2, 0, 1), children.T, octant, far_slot.T, far_offset.T, far_count.reshape(1, boxes),
        pat, *halves(phi_matrix().T), *halves(theta_blocks(n_dir)), jnp.asarray(phase_tables()), tr,
    )
    received_shape = jax.ShapeDtypeStruct((boxes, 8, 128), f32)
    upward_shape = jax.ShapeDtypeStruct((n_dir, 2, 16, 128), f32)
    row_shape = jax.ShapeDtypeStruct((n_far, boxes), i32)
    src, tc, row_s, row_t, upward = pl.pallas_call(
        functools.partial(kernel, n_box, n_dir, n_send, boxes, n_tr, n_far),
        out_shape=(
            jax.ShapeDtypeStruct((n_box * n_send * 8, 128), f32),
            jax.ShapeDtypeStruct((n_tr * 8 + 8, 128), f32),
            row_shape, row_shape, upward_shape,
        ),
        in_specs=[hbm] * len(operands),
        out_specs=(vmem,) * 5,
        scratch_shapes=[
            pltpu.SMEM((n_send, 1, n_box), i32), pltpu.SMEM((CH, n_dir), i32), pltpu.SMEM((boxes,), i32),
            pltpu.VMEM((boxes, 8, 128), f32),
            pltpu.VMEM((PHI0, PHI1), bf16), pltpu.VMEM((PHI0, PHI1), bf16),
            pltpu.VMEM((2 * THETA1, 128), bf16), pltpu.VMEM((2 * THETA1, 128), bf16),
            pltpu.VMEM((4, 2, THETA1, PHI1), f32),
            pltpu.VMEM((n_tr * 8, 128), f32),
            pltpu.VMEM((n_far, boxes), i32), pltpu.VMEM((n_far, boxes), i32), pltpu.VMEM((1, boxes), i32),
            pltpu.VMEM((n_box * n_send * 8, 128), f32),
            pltpu.VMEM((n_dir, CH, 8, 128), f32),
            pltpu.VMEM((n_dir, CH, 8, 128), f32),
            pltpu.VMEM((CH, 2 * THETA1, PHI1), f32),
            pltpu.VMEM((n_dir, 2, 16, 128), f32),
            dma((1,)), dma((1,)), dma((1,)), dma((1,)), dma((1,)), dma((1,)),
            dma((15,)),
        ],
        compiler_params=pltpu.CompilerParams(
            collective_id=0, has_side_effects=True, vmem_limit_bytes=24 << 20
        ),
        name="exchange",
    )(*(pltpu.with_memory_space_constraint(x, pltpu.HBM) for x in operands))
    received, upward = pl.pallas_call(
        functools.partial(far_kernel, n_far, boxes),
        out_shape=(received_shape, upward_shape),
        in_specs=[smem, smem, vmem, vmem, vmem],
        out_specs=(hbm, hbm),
        scratch_shapes=[pltpu.VMEM((boxes, 8, 128), f32), dma((1 + boxes // PIECE,))],
        compiler_params=pltpu.CompilerParams(vmem_limit_bytes=8 << 20),
        name="far",
    )(row_s, row_t, src, tc, upward)
    return received.reshape(patterns.shape), upward.reshape(children.shape[0], 2, 1, -1)


def solution(mesh):
    return jax.shard_map(
        shards,
        mesh=mesh,
        in_specs=(
            P("box", None, None, "dir"),
            P(None, None, "dir"),
            P("box", None, None),
            P("box", None),
            P("box", None),
            P("box"),
            P("box", None),
            P("box"),
        ),
        out_specs=(P("box", None, None, "dir"), P("box", None, None, "dir")),
        check_vma=False,
    )
```

```python
import functools

import jax
import jax.numpy as jnp
import numpy as np
from jax import lax
from jax.experimental import pallas as pl
from jax.experimental.pallas import tpu as pltpu
from jax.sharding import PartitionSpec as P

THETA0 = 64
PHI0 = 128
THETA1 = 128
PHI1 = 256
CH = 4
HALF_PHASE = 8.0
MESH = pl.DeviceIdType.MESH
PIECE = 16


def theta_matrix():
    fine = np.pi * (np.arange(THETA1) + 0.5) / THETA1
    coarse = np.pi * (np.arange(THETA0) + 0.5) / THETA0
    orders = np.arange(THETA0)
    weights = np.where(orders > 0, 2.0, 1.0)
    return (np.cos(fine[:, None] * orders) * weights) @ np.cos(coarse[:, None] * orders).T / THETA0


def phi_matrix():
    fine = 2.0 * np.pi * np.arange(PHI1) / PHI1
    coarse = 2.0 * np.pi * np.arange(PHI0) / PHI0
    orders = np.arange(PHI0 // 2 + 1)
    weights = np.where((orders == 0) | (orders == PHI0 // 2), 1.0, 2.0)
    delta = fine[:, None] - coarse[None, :]
    return np.sum(weights * np.cos(delta[:, :, None] * orders), axis=-1) / PHI0


def phase_tables():
    theta = np.pi * (np.arange(THETA1) + 0.5) / THETA1
    phi = 2.0 * np.pi * np.arange(PHI1) / PHI1
    ux = np.sin(theta)[:, None] * np.cos(phi)[None, :]
    uy = np.sin(theta)[:, None] * np.sin(phi)[None, :]
    uz = np.cos(theta)[:, None] * np.ones((1, PHI1))
    tables = []
    for o in range(4):
        sx, sy = 1.0 - 2.0 * (o % 2), 1.0 - 2.0 * (o // 2 % 2)
        angle = HALF_PHASE * (sx * ux + sy * uy + uz)
        tables.append(np.stack([np.cos(angle), np.sin(angle)]))
    return np.stack(tables).astype(np.float32)


def theta_blocks(n_dir):
    rows = THETA0 // n_dir
    m = theta_matrix().reshape(THETA1, n_dir, rows)
    out = np.zeros((2, THETA1, n_dir, 2, rows))
    for part in range(2):
        out[part, :, :, part, :] = m
    return out.reshape(2 * THETA1, n_dir * 2 * rows)


def halves(x):
    hi = jnp.asarray(x, jnp.float32).astype(jnp.bfloat16)
    lo = (jnp.asarray(x, jnp.float32) - hi.astype(jnp.float32)).astype(jnp.bfloat16)
    return hi, lo


def dot3(ah, al, bh, bl):
    dot = functools.partial(jnp.dot, preferred_element_type=jnp.float32)
    return dot(ah, bh) + (dot(al, bh) + dot(ah, bl))


def kernel(
    n_box, n_dir, n_send, boxes, n_tr, n_far,
    send_hbm, child_hbm, oct_hbm, slot_hbm, off_hbm, cnt_hbm, pat_hbm, ph_hbm, pl_hbm, mh_hbm, ml_hbm, tab_hbm, tr_hbm,
    src, tc, row_s, row_t, up_out,
    send_ref, child_ref, oct_ref, pat, ph, plo, mh, mlo, tab, tr, slot, off, cnt,
    box_buf, dir_buf, dir_in, z_buf, up_buf,
    box_send, box_recv, dir_send, dir_recv, up_send, up_recv, sem, ready,
):
    box = lax.axis_index("box")
    here = lax.axis_index("dir")
    rows = 8 * n_send
    barrier = pltpu.get_barrier_semaphore()

    def local(k, source, target):
        copy = pltpu.make_async_copy(source, target, sem.at[k])
        copy.start()
        return copy

    first = [
        local(0, send_hbm, send_ref), local(1, pat_hbm, pat), local(2, child_hbm, child_ref),
    ]

    levels, lines = n_box // 4, n_dir // 2
    level, spot = box // 4, lax.rem(box, 4)
    side, line = here // lines, lax.rem(here, lines)
    spots = [lax.rem(spot + j, 4) for j in range(4)]
    sides = [lax.rem(side + j, 2) * lines for j in range(2)]

    def far_first(k, n):
        return n // 2 + (1 - 2 * lax.rem(k, 2)) * ((k + 1) // 2)

    def base(step):
        return lax.rem(level + step, levels) * 4

    def each_at(steps, visit):
        @pl.loop(0, 4)
        def _(j):
            for step in steps:
                visit(base(step) + lax.rem(spot + 2 + j, 4))

    def each_near(visit):
        each_at((1, levels - 1), visit)
        for j in (2, 3, 1):
            visit(level * 4 + spots[j])

    def each_dir(visit):
        @pl.loop(0, lines - 1)
        def _(k):
            step = far_first(k, lines)
            at = lax.rem(line + step, lines)
            for j in (1, 0):
                visit(sides[j] + at)

        visit(sides[1] + line)

    def greet(axis, to):
        pl.semaphore_signal(barrier, inc=1, device_id={axis: to}, device_id_type=MESH)

    each_near(lambda to: greet("box", to))
    each_dir(lambda to: greet("dir", to))

    later = [
        local(3, oct_hbm, oct_ref), local(4, ph_hbm, ph), local(5, pl_hbm, plo), local(6, mh_hbm, mh),
        local(7, ml_hbm, mlo), local(8, tab_hbm, tab),
    ]
    tables = [
        local(9, tr_hbm, tr), local(10, slot_hbm, slot), local(11, off_hbm, off), local(12, cnt_hbm, cnt),
    ]

    for copy in first:
        copy.wait()

    @pl.loop(0, n_box // 4)
    def _(k):
        for r in range(4):
            for j in range(n_send):
                at = pl.multiple_of((4 * k + r) * rows + j * 8, 8)
                box_buf[pl.ds(at, 8), :] = pat[send_ref[j, 0, 4 * k + r]]

    def child(c, r):
        return jnp.maximum(child_ref[c, r] - box * boxes, 0)

    @pl.loop(0, n_dir // 2)
    def _(k):
        for r in range(2):
            for c in range(CH):
                dir_buf[2 * k + r, c] = pat[child(c, 2 * k + r)]

    pl.semaphore_wait(barrier, n_dir - 1 + 11)

    def announce(k, step):
        pl.semaphore_signal(
            ready.at[k], inc=1, device_id={"box": base(step) + spot}, device_id_type=MESH
        )

    up_one, down_one = 1, levels - 1
    announce(0, down_one)
    announce(1, up_one)

    def dir_copy(to):
        return pltpu.make_async_remote_copy(
            src_ref=dir_buf.at[to], dst_ref=dir_in.at[here],
            send_sem=dir_send.at[0], recv_sem=dir_recv.at[0],
            device_id={"dir": to}, device_id_type=MESH,
        )

    def box_copy(to):
        return pltpu.make_async_remote_copy(
            src_ref=box_buf.at[pl.ds(pl.multiple_of(to * rows, 8), rows)],
            dst_ref=src.at[pl.ds(pl.multiple_of(box * rows, 8), rows)],
            send_sem=box_send.at[0], recv_sem=box_recv.at[0],
            device_id={"box": to}, device_id_type=MESH,
        )

    def up_copy(to):
        return pltpu.make_async_remote_copy(
            src_ref=up_buf.at[to], dst_ref=up_out.at[here],
            send_sem=up_send.at[0], recv_sem=up_recv.at[0],
            device_id={"dir": to}, device_id_type=MESH,
        )

    each_dir(lambda to: dir_copy(to).start())

    def send(to):
        box_copy(to).start()

    each_near(send)
    pl.semaphore_wait(ready.at[0], 1)
    announce(2, down_one)
    pl.semaphore_wait(ready.at[1], 1)
    announce(3, up_one)
    each_at((2, levels - 2), send)
    pl.semaphore_wait(ready.at[2], 1)
    announce(4, down_one)
    pl.semaphore_wait(ready.at[3], 1)
    each_at((3, levels - 3), send)
    pl.semaphore_wait(ready.at[4], 1)
    each_at((4,), send)

    def all_of(source, target, send_sem, recv_sem):
        return pltpu.make_async_remote_copy(
            src_ref=source, dst_ref=target, send_sem=send_sem.at[0], recv_sem=recv_sem.at[0],
            device_id={"box": lax.rem(box + 1, n_box)}, device_id_type=MESH,
        )

    all_dir = all_of(
        dir_buf.at[pl.ds(0, n_dir - 1)], dir_in.at[pl.ds(0, n_dir - 1)], dir_send, dir_recv
    )
    all_up = all_of(up_buf.at[pl.ds(0, n_dir - 1)], up_out.at[pl.ds(0, n_dir - 1)], up_send, up_recv)
    all_box = all_of(
        box_buf.at[pl.ds(0, (n_box - 1) * rows)], src.at[pl.ds(0, (n_box - 1) * rows)], box_send, box_recv
    )

    for c in range(CH):
        dir_in[here, c] = pat[child(c, here)]

    for j in range(n_send):
        src[pl.ds(pl.multiple_of(box * rows + j * 8, 8), 8), :] = pat[send_ref[j, 0, box]]

    for copy in tables:
        copy.wait()
    low = lax.broadcasted_iota(jnp.int32, (8, 128), 0) < 4

    @pl.loop(0, n_tr // 2)
    def _(k):
        at = pl.multiple_of(k * 16, 16)
        re = tr[pl.ds(at, 8, stride=2), :]
        im = tr[pl.ds(at + 1, 8, stride=2), :]
        tc[pl.ds(at, 8), :] = jnp.where(low, re, pltpu.roll(im, 4, 0))
        tc[pl.ds(at + 8, 8), :] = jnp.where(low, pltpu.roll(re, 4, 0), im)

    tc[pl.ds(n_tr * 8, 8), :] = jnp.zeros((8, 128), jnp.float32)

    live = lax.broadcasted_iota(jnp.int32, (n_far, boxes), 0) < cnt[...]
    row_s[...] = slot[...] * 8
    row_t[...] = jnp.where(live, off[...], n_tr) * 8

    all_dir.wait_recv()

    for copy in later:
        copy.wait()

    for c in range(CH):
        x = dir_in[:, c].reshape(n_dir * 8, 128)
        y = dot3(*halves(x), ph[...], plo[...])
        z_buf[c] = dot3(mh[...], mlo[...], *halves(y))

    octants = [oct_ref[child(c, here)] for c in range(CH)]
    table = [jnp.where(o < 4, o, 7 - o) for o in octants]
    sign = [jnp.where(o < 4, 1.0, -1.0).astype(jnp.float32) for o in octants]

    @pl.loop(0, n_dir)
    def _(r):
        at = pl.multiple_of(r * 8, 8)
        for half in range(2):
            cols = pl.ds(half * 128, 128)
            re = im = None
            for c in range(CH):
                zr = z_buf[c, pl.ds(at, 8), cols]
                zi = z_buf[c, pl.ds(at + THETA1, 8), cols]
                cos = tab[table[c], 0, pl.ds(at, 8), cols]
                sin = tab[table[c], 1, pl.ds(at, 8), cols] * sign[c]
                a, b = zr * cos - zi * sin, zr * sin + zi * cos
                re, im = (a, b) if c == 0 else (re + a, im + b)
            up_buf[r, 0, pl.ds(half, 8, stride=2), :] = re
            up_buf[r, 1, pl.ds(half, 8, stride=2), :] = im

    each_dir(lambda to: up_copy(to).start())

    own_up = local(14, up_buf.at[here], up_out.at[here])

    all_dir.wait_send()

    own_up.wait()


    all_box.wait_recv()

    all_up.wait()

    all_box.wait_send()


def far_kernel(n_far, boxes, row_s, row_t, src, tc, up, far_out, up_out, held, sem):
    up_copy = pltpu.make_async_copy(up, up_out, sem.at[0])
    up_copy.start()
    low = lax.broadcasted_iota(jnp.int32, (8, 128), 0) < 4
    copies = []
    for b in range(boxes):
        p, q = [None, None], [None, None]
        for f in range(n_far):
            t = tc[pl.ds(pl.multiple_of(row_t[f, b], 8), 8), :]
            a = src[pl.ds(pl.multiple_of(row_s[f, b], 8), 8), :]
            u, v = a * t, pltpu.roll(a, 4, 0) * t
            k = f % 2
            p[k], q[k] = (u, v) if f < 2 else (p[k] + u, q[k] + v)
        p, q = p[0] + p[1], q[0] + q[1]
        held[b] = jnp.where(low, p - pltpu.roll(p, 4, 0), q + pltpu.roll(q, 4, 0))
        if b % PIECE == PIECE - 1:
            part = pl.ds(b + 1 - PIECE, PIECE)
            copies.append(pltpu.make_async_copy(held.at[part], far_out.at[part], sem.at[1 + b // PIECE]))
            copies[-1].start()
    for copy in [up_copy] + copies:
        copy.wait()


def shards(patterns, translators, send_rows, far_slot, far_offset, far_count, children, octant):
    n_box, n_dir = lax.axis_size("box"), lax.axis_size("dir")
    boxes, n_send = patterns.shape[0], send_rows.shape[2]
    n_tr, n_far = translators.shape[0], far_slot.shape[1]
    pat = patterns.reshape(boxes, 8, 128)
    tr = translators.reshape(n_tr, 2, 4, 128).transpose(0, 2, 1, 3).reshape(n_tr * 8, 128)
    vmem, smem = pl.BlockSpec(memory_space=pltpu.VMEM), pl.BlockSpec(memory_space=pltpu.SMEM)
    hbm = pl.BlockSpec(memory_space=pltpu.HBM)
    f32, i32, bf16 = jnp.float32, jnp.int32, jnp.bfloat16
    dma = pltpu.SemaphoreType.DMA
    operands = (
        send_rows.transpose(2, 0, 1), children.T, octant, far_slot.T, far_offset.T, far_count.reshape(1, boxes),
        pat, *halves(phi_matrix().T), *halves(theta_blocks(n_dir)), jnp.asarray(phase_tables()), tr,
    )
    received_shape = jax.ShapeDtypeStruct((boxes, 8, 128), f32)
    upward_shape = jax.ShapeDtypeStruct((n_dir, 2, 16, 128), f32)
    row_shape = jax.ShapeDtypeStruct((n_far, boxes), i32)
    src, tc, row_s, row_t, upward = pl.pallas_call(
        functools.partial(kernel, n_box, n_dir, n_send, boxes, n_tr, n_far),
        out_shape=(
            jax.ShapeDtypeStruct((n_box * n_send * 8, 128), f32),
            jax.ShapeDtypeStruct((n_tr * 8 + 8, 128), f32),
            row_shape, row_shape, upward_shape,
        ),
        in_specs=[hbm] * len(operands),
        out_specs=(vmem,) * 5,
        scratch_shapes=[
            pltpu.SMEM((n_send, 1, n_box), i32), pltpu.SMEM((CH, n_dir), i32), pltpu.SMEM((boxes,), i32),
            pltpu.VMEM((boxes, 8, 128), f32),
            pltpu.VMEM((PHI0, PHI1), bf16), pltpu.VMEM((PHI0, PHI1), bf16),
            pltpu.VMEM((2 * THETA1, 128), bf16), pltpu.VMEM((2 * THETA1, 128), bf16),
            pltpu.VMEM((4, 2, THETA1, PHI1), f32),
            pltpu.VMEM((n_tr * 8, 128), f32),
            pltpu.VMEM((n_far, boxes), i32), pltpu.VMEM((n_far, boxes), i32), pltpu.VMEM((1, boxes), i32),
            pltpu.VMEM((n_box * n_send * 8, 128), f32),
            pltpu.VMEM((n_dir, CH, 8, 128), f32),
            pltpu.VMEM((n_dir, CH, 8, 128), f32),
            pltpu.VMEM((CH, 2 * THETA1, PHI1), f32),
            pltpu.VMEM((n_dir, 2, 16, 128), f32),
            dma((1,)), dma((1,)), dma((1,)), dma((1,)), dma((1,)), dma((1,)),
            dma((15,)), pltpu.SemaphoreType.REGULAR((5,)),
        ],
        compiler_params=pltpu.CompilerParams(
            collective_id=0, has_side_effects=True, vmem_limit_bytes=24 << 20
        ),
        name="exchange",
    )(*(pltpu.with_memory_space_constraint(x, pltpu.HBM) for x in operands))
    received, upward = pl.pallas_call(
        functools.partial(far_kernel, n_far, boxes),
        out_shape=(received_shape, upward_shape),
        in_specs=[smem, smem, vmem, vmem, vmem],
        out_specs=(hbm, hbm),
        scratch_shapes=[pltpu.VMEM((boxes, 8, 128), f32), dma((1 + boxes // PIECE,))],
        compiler_params=pltpu.CompilerParams(vmem_limit_bytes=8 << 20),
        name="far",
    )(row_s, row_t, src, tc, upward)
    return received.reshape(patterns.shape), upward.reshape(children.shape[0], 2, 1, -1)


def solution(mesh):
    return jax.shard_map(
        shards,
        mesh=mesh,
        in_specs=(
            P("box", None, None, "dir"),
            P(None, None, "dir"),
            P("box", None, None),
            P("box", None),
            P("box", None),
            P("box"),
            P("box", None),
            P("box"),
        ),
        out_specs=(P("box", None, None, "dir"), P("box", None, None, "dir")),
        check_vma=False,
    )
```

```python
import functools

import jax
import jax.numpy as jnp
import numpy as np
from jax import lax
from jax.experimental import pallas as pl
from jax.experimental.pallas import tpu as pltpu
from jax.sharding import PartitionSpec as P

THETA0 = 64
PHI0 = 128
THETA1 = 128
PHI1 = 256
CH = 4
HALF_PHASE = 8.0
MESH = pl.DeviceIdType.MESH
PIECE = 16


def theta_matrix():
    fine = np.pi * (np.arange(THETA1) + 0.5) / THETA1
    coarse = np.pi * (np.arange(THETA0) + 0.5) / THETA0
    orders = np.arange(THETA0)
    weights = np.where(orders > 0, 2.0, 1.0)
    return (np.cos(fine[:, None] * orders) * weights) @ np.cos(coarse[:, None] * orders).T / THETA0


def phi_matrix():
    fine = 2.0 * np.pi * np.arange(PHI1) / PHI1
    coarse = 2.0 * np.pi * np.arange(PHI0) / PHI0
    orders = np.arange(PHI0 // 2 + 1)
    weights = np.where((orders == 0) | (orders == PHI0 // 2), 1.0, 2.0)
    delta = fine[:, None] - coarse[None, :]
    return np.sum(weights * np.cos(delta[:, :, None] * orders), axis=-1) / PHI0


def phase_tables():
    theta = np.pi * (np.arange(THETA1) + 0.5) / THETA1
    phi = 2.0 * np.pi * np.arange(PHI1) / PHI1
    ux = np.sin(theta)[:, None] * np.cos(phi)[None, :]
    uy = np.sin(theta)[:, None] * np.sin(phi)[None, :]
    uz = np.cos(theta)[:, None] * np.ones((1, PHI1))
    tables = []
    for o in range(4):
        sx, sy = 1.0 - 2.0 * (o % 2), 1.0 - 2.0 * (o // 2 % 2)
        angle = HALF_PHASE * (sx * ux + sy * uy + uz)
        tables.append(np.stack([np.cos(angle), np.sin(angle)]))
    return np.stack(tables).astype(np.float32)


def theta_blocks(n_dir):
    rows = THETA0 // n_dir
    m = theta_matrix().reshape(THETA1, n_dir, rows)
    out = np.zeros((2, THETA1, n_dir, 2, rows))
    for part in range(2):
        out[part, :, :, part, :] = m
    return out.reshape(2 * THETA1, n_dir * 2 * rows)


def halves(x):
    hi = jnp.asarray(x, jnp.float32).astype(jnp.bfloat16)
    lo = (jnp.asarray(x, jnp.float32) - hi.astype(jnp.float32)).astype(jnp.bfloat16)
    return hi, lo


def dot3(ah, al, bh, bl):
    dot = functools.partial(jnp.dot, preferred_element_type=jnp.float32)
    return dot(ah, bh) + (dot(al, bh) + dot(ah, bl))


def kernel(
    n_box, n_dir, n_send, boxes, n_tr, n_far,
    send_hbm, child_hbm, oct_hbm, slot_hbm, off_hbm, cnt_hbm, pat_hbm, ph_hbm, pl_hbm, mh_hbm, ml_hbm, tab_hbm, tr_hbm,
    src, tc, row_s, row_t, up_out,
    send_ref, child_ref, oct_ref, pat, ph, plo, mh, mlo, tab, tr, slot, off, cnt,
    box_buf, dir_buf, dir_in, z_buf, up_buf,
    box_send, box_recv, dir_send, dir_recv, up_send, up_recv, sem, ready,
):
    box = lax.axis_index("box")
    here = lax.axis_index("dir")
    rows = 8 * n_send
    barrier = pltpu.get_barrier_semaphore()

    def local(k, source, target):
        copy = pltpu.make_async_copy(source, target, sem.at[k])
        copy.start()
        return copy

    first = [
        local(0, send_hbm, send_ref), local(1, pat_hbm, pat), local(2, child_hbm, child_ref),
    ]

    levels, lines = n_box // 4, n_dir // 2
    level, spot = box // 4, lax.rem(box, 4)
    side, line = here // lines, lax.rem(here, lines)
    spots = [lax.rem(spot + j, 4) for j in range(4)]
    sides = [lax.rem(side + j, 2) * lines for j in range(2)]

    def far_first(k, n):
        return n // 2 + (1 - 2 * lax.rem(k, 2)) * ((k + 1) // 2)

    def base(step):
        return lax.rem(level + step, levels) * 4

    def each_at(steps, visit):
        @pl.loop(0, 4)
        def _(j):
            for step in steps:
                visit(base(step) + lax.rem(spot + 2 + j, 4))

    def each_near(visit):
        each_at((1, levels - 1), visit)
        for j in (2, 3, 1):
            visit(level * 4 + spots[j])

    def across(step):
        return lax.rem(line + step, lines)

    def each_line(steps, visit):
        @pl.loop(0, 2)
        def _(j):
            for step in steps:
                visit(lax.rem(side + 1 + j, 2) * lines + across(step))

    def near_dir(visit):
        each_line((1, lines - 1), visit)
        visit(sides[1] + line)

    def each_dir(visit):
        @pl.loop(0, lines - 1)
        def _(k):
            at = across(far_first(k, lines))
            for j in (1, 0):
                visit(sides[j] + at)

        visit(sides[1] + line)

    def greet(axis, to):
        pl.semaphore_signal(barrier, inc=1, device_id={axis: to}, device_id_type=MESH)

    each_near(lambda to: greet("box", to))
    near_dir(lambda to: greet("dir", to))

    later = [
        local(3, oct_hbm, oct_ref), local(4, ph_hbm, ph), local(5, pl_hbm, plo), local(6, mh_hbm, mh),
        local(7, ml_hbm, mlo), local(8, tab_hbm, tab),
    ]
    tables = [
        local(9, tr_hbm, tr), local(10, slot_hbm, slot), local(11, off_hbm, off), local(12, cnt_hbm, cnt),
    ]

    for copy in first:
        copy.wait()

    @pl.loop(0, n_box // 4)
    def _(k):
        for r in range(4):
            for j in range(n_send):
                at = pl.multiple_of((4 * k + r) * rows + j * 8, 8)
                box_buf[pl.ds(at, 8), :] = pat[send_ref[j, 0, 4 * k + r]]

    def child(c, r):
        return jnp.maximum(child_ref[c, r] - box * boxes, 0)

    @pl.loop(0, n_dir // 2)
    def _(k):
        for r in range(2):
            for c in range(CH):
                dir_buf[2 * k + r, c] = pat[child(c, 2 * k + r)]

    pl.semaphore_wait(barrier, 5 + 11)

    def announce(k, step):
        pl.semaphore_signal(
            ready.at[k], inc=1, device_id={"box": base(step) + spot}, device_id_type=MESH
        )

    def announce_dir(k, step):
        pl.semaphore_signal(
            ready.at[5 + k], inc=1, device_id={"dir": sides[0] + across(step)}, device_id_type=MESH
        )

    def heard(k):
        pl.semaphore_wait(ready.at[k], 1)

    up_one, down_one = 1, levels - 1
    right, left = 1, lines - 1
    announce(0, down_one)
    announce(1, up_one)
    announce_dir(0, left)
    announce_dir(1, right)

    def dir_copy(to):
        return pltpu.make_async_remote_copy(
            src_ref=dir_buf.at[to], dst_ref=dir_in.at[here],
            send_sem=dir_send.at[0], recv_sem=dir_recv.at[0],
            device_id={"dir": to}, device_id_type=MESH,
        )

    def box_copy(to):
        return pltpu.make_async_remote_copy(
            src_ref=box_buf.at[pl.ds(pl.multiple_of(to * rows, 8), rows)],
            dst_ref=src.at[pl.ds(pl.multiple_of(box * rows, 8), rows)],
            send_sem=box_send.at[0], recv_sem=box_recv.at[0],
            device_id={"box": to}, device_id_type=MESH,
        )

    def up_copy(to):
        return pltpu.make_async_remote_copy(
            src_ref=up_buf.at[to], dst_ref=up_out.at[here],
            send_sem=up_send.at[0], recv_sem=up_recv.at[0],
            device_id={"dir": to}, device_id_type=MESH,
        )


    def send(to):
        box_copy(to).start()

    def send_dir(to):
        dir_copy(to).start()

    each_near(send)
    near_dir(send_dir)
    heard(0)
    announce(2, down_one)
    heard(1)
    announce(3, up_one)
    heard(5)
    announce_dir(2, left)
    heard(6)
    announce_dir(3, right)
    each_at((2, levels - 2), send)
    each_line((2, lines - 2), send_dir)
    heard(2)
    announce(4, down_one)
    heard(3)
    heard(7)
    announce_dir(4, left)
    heard(8)
    each_at((3, levels - 3), send)
    each_line((3, lines - 3), send_dir)
    heard(4)
    each_at((4,), send)
    heard(9)
    each_line((4,), send_dir)

    def all_of(source, target, send_sem, recv_sem):
        return pltpu.make_async_remote_copy(
            src_ref=source, dst_ref=target, send_sem=send_sem.at[0], recv_sem=recv_sem.at[0],
            device_id={"box": lax.rem(box + 1, n_box)}, device_id_type=MESH,
        )

    all_dir = all_of(
        dir_buf.at[pl.ds(0, n_dir - 1)], dir_in.at[pl.ds(0, n_dir - 1)], dir_send, dir_recv
    )
    all_up = all_of(up_buf.at[pl.ds(0, n_dir - 1)], up_out.at[pl.ds(0, n_dir - 1)], up_send, up_recv)
    all_box = all_of(
        box_buf.at[pl.ds(0, (n_box - 1) * rows)], src.at[pl.ds(0, (n_box - 1) * rows)], box_send, box_recv
    )

    for c in range(CH):
        dir_in[here, c] = pat[child(c, here)]

    for j in range(n_send):
        src[pl.ds(pl.multiple_of(box * rows + j * 8, 8), 8), :] = pat[send_ref[j, 0, box]]

    for copy in tables:
        copy.wait()
    low = lax.broadcasted_iota(jnp.int32, (8, 128), 0) < 4

    @pl.loop(0, n_tr // 2)
    def _(k):
        at = pl.multiple_of(k * 16, 16)
        re = tr[pl.ds(at, 8, stride=2), :]
        im = tr[pl.ds(at + 1, 8, stride=2), :]
        tc[pl.ds(at, 8), :] = jnp.where(low, re, pltpu.roll(im, 4, 0))
        tc[pl.ds(at + 8, 8), :] = jnp.where(low, pltpu.roll(re, 4, 0), im)

    tc[pl.ds(n_tr * 8, 8), :] = jnp.zeros((8, 128), jnp.float32)

    live = lax.broadcasted_iota(jnp.int32, (n_far, boxes), 0) < cnt[...]
    row_s[...] = slot[...] * 8
    row_t[...] = jnp.where(live, off[...], n_tr) * 8

    all_dir.wait_recv()

    for copy in later:
        copy.wait()

    for c in range(CH):
        x = dir_in[:, c].reshape(n_dir * 8, 128)
        y = dot3(*halves(x), ph[...], plo[...])
        z_buf[c] = dot3(mh[...], mlo[...], *halves(y))

    octants = [oct_ref[child(c, here)] for c in range(CH)]
    table = [jnp.where(o < 4, o, 7 - o) for o in octants]
    sign = [jnp.where(o < 4, 1.0, -1.0).astype(jnp.float32) for o in octants]

    @pl.loop(0, n_dir)
    def _(r):
        at = pl.multiple_of(r * 8, 8)
        for half in range(2):
            cols = pl.ds(half * 128, 128)
            re = im = None
            for c in range(CH):
                zr = z_buf[c, pl.ds(at, 8), cols]
                zi = z_buf[c, pl.ds(at + THETA1, 8), cols]
                cos = tab[table[c], 0, pl.ds(at, 8), cols]
                sin = tab[table[c], 1, pl.ds(at, 8), cols] * sign[c]
                a, b = zr * cos - zi * sin, zr * sin + zi * cos
                re, im = (a, b) if c == 0 else (re + a, im + b)
            up_buf[r, 0, pl.ds(half, 8, stride=2), :] = re
            up_buf[r, 1, pl.ds(half, 8, stride=2), :] = im

    each_dir(lambda to: up_copy(to).start())

    own_up = local(14, up_buf.at[here], up_out.at[here])

    all_dir.wait_send()

    own_up.wait()


    all_box.wait_recv()

    all_up.wait()

    all_box.wait_send()


def far_kernel(n_far, boxes, row_s, row_t, src, tc, up, far_out, up_out, held, sem):
    up_copy = pltpu.make_async_copy(up, up_out, sem.at[0])
    up_copy.start()
    low = lax.broadcasted_iota(jnp.int32, (8, 128), 0) < 4
    copies = []
    for b in range(boxes):
        p, q = [None, None], [None, None]
        for f in range(n_far):
            t = tc[pl.ds(pl.multiple_of(row_t[f, b], 8), 8), :]
            a = src[pl.ds(pl.multiple_of(row_s[f, b], 8), 8), :]
            u, v = a * t, pltpu.roll(a, 4, 0) * t
            k = f % 2
            p[k], q[k] = (u, v) if f < 2 else (p[k] + u, q[k] + v)
        p, q = p[0] + p[1], q[0] + q[1]
        held[b] = jnp.where(low, p - pltpu.roll(p, 4, 0), q + pltpu.roll(q, 4, 0))
        if b % PIECE == PIECE - 1:
            part = pl.ds(b + 1 - PIECE, PIECE)
            copies.append(pltpu.make_async_copy(held.at[part], far_out.at[part], sem.at[1 + b // PIECE]))
            copies[-1].start()
    for copy in [up_copy] + copies:
        copy.wait()


def shards(patterns, translators, send_rows, far_slot, far_offset, far_count, children, octant):
    n_box, n_dir = lax.axis_size("box"), lax.axis_size("dir")
    boxes, n_send = patterns.shape[0], send_rows.shape[2]
    n_tr, n_far = translators.shape[0], far_slot.shape[1]
    pat = patterns.reshape(boxes, 8, 128)
    tr = translators.reshape(n_tr, 2, 4, 128).transpose(0, 2, 1, 3).reshape(n_tr * 8, 128)
    vmem, smem = pl.BlockSpec(memory_space=pltpu.VMEM), pl.BlockSpec(memory_space=pltpu.SMEM)
    hbm = pl.BlockSpec(memory_space=pltpu.HBM)
    f32, i32, bf16 = jnp.float32, jnp.int32, jnp.bfloat16
    dma = pltpu.SemaphoreType.DMA
    operands = (
        send_rows.transpose(2, 0, 1), children.T, octant, far_slot.T, far_offset.T, far_count.reshape(1, boxes),
        pat, *halves(phi_matrix().T), *halves(theta_blocks(n_dir)), jnp.asarray(phase_tables()), tr,
    )
    received_shape = jax.ShapeDtypeStruct((boxes, 8, 128), f32)
    upward_shape = jax.ShapeDtypeStruct((n_dir, 2, 16, 128), f32)
    row_shape = jax.ShapeDtypeStruct((n_far, boxes), i32)
    src, tc, row_s, row_t, upward = pl.pallas_call(
        functools.partial(kernel, n_box, n_dir, n_send, boxes, n_tr, n_far),
        out_shape=(
            jax.ShapeDtypeStruct((n_box * n_send * 8, 128), f32),
            jax.ShapeDtypeStruct((n_tr * 8 + 8, 128), f32),
            row_shape, row_shape, upward_shape,
        ),
        in_specs=[hbm] * len(operands),
        out_specs=(vmem,) * 5,
        scratch_shapes=[
            pltpu.SMEM((n_send, 1, n_box), i32), pltpu.SMEM((CH, n_dir), i32), pltpu.SMEM((boxes,), i32),
            pltpu.VMEM((boxes, 8, 128), f32),
            pltpu.VMEM((PHI0, PHI1), bf16), pltpu.VMEM((PHI0, PHI1), bf16),
            pltpu.VMEM((2 * THETA1, 128), bf16), pltpu.VMEM((2 * THETA1, 128), bf16),
            pltpu.VMEM((4, 2, THETA1, PHI1), f32),
            pltpu.VMEM((n_tr * 8, 128), f32),
            pltpu.VMEM((n_far, boxes), i32), pltpu.VMEM((n_far, boxes), i32), pltpu.VMEM((1, boxes), i32),
            pltpu.VMEM((n_box * n_send * 8, 128), f32),
            pltpu.VMEM((n_dir, CH, 8, 128), f32),
            pltpu.VMEM((n_dir, CH, 8, 128), f32),
            pltpu.VMEM((CH, 2 * THETA1, PHI1), f32),
            pltpu.VMEM((n_dir, 2, 16, 128), f32),
            dma((1,)), dma((1,)), dma((1,)), dma((1,)), dma((1,)), dma((1,)),
            dma((15,)), pltpu.SemaphoreType.REGULAR((10,)),
        ],
        compiler_params=pltpu.CompilerParams(
            collective_id=0, has_side_effects=True, vmem_limit_bytes=24 << 20
        ),
        name="exchange",
    )(*(pltpu.with_memory_space_constraint(x, pltpu.HBM) for x in operands))
    received, upward = pl.pallas_call(
        functools.partial(far_kernel, n_far, boxes),
        out_shape=(received_shape, upward_shape),
        in_specs=[smem, smem, vmem, vmem, vmem],
        out_specs=(hbm, hbm),
        scratch_shapes=[pltpu.VMEM((boxes, 8, 128), f32), dma((1 + boxes // PIECE,))],
        compiler_params=pltpu.CompilerParams(vmem_limit_bytes=8 << 20),
        name="far",
    )(row_s, row_t, src, tc, upward)
    return received.reshape(patterns.shape), upward.reshape(children.shape[0], 2, 1, -1)


def solution(mesh):
    return jax.shard_map(
        shards,
        mesh=mesh,
        in_specs=(
            P("box", None, None, "dir"),
            P(None, None, "dir"),
            P("box", None, None),
            P("box", None),
            P("box", None),
            P("box"),
            P("box", None),
            P("box"),
        ),
        out_specs=(P("box", None, None, "dir"), P("box", None, None, "dir")),
        check_vma=False,
    )
```
